256 devices in a mesh: row: 32 (over z, y), col: 8 (over x, core).
Axes of the slice: x: 4, y: 4, z: 8, core: 2. Of those that a mesh axis runs over, the one named last changes fastest.
Arguments:
- inputs: bfloat16 [16384, 2048], P('row', 'col'), may hold values from -6 to 6
- grad_out: bfloat16 [16384, 2048], P('row', 'col'), may hold values from -6 to 6
- gate_pre: bfloat16 [16384, 7168], P('row', 'col'), may hold values from -8 to 8
- up_pre: bfloat16 [16384, 7168], P('row', 'col'), may hold values from -6 to 6
- gate_weight: bfloat16 [2048, 7168], P('row', 'col'), may hold values from -0.125 to 0.125
- up_weight: bfloat16 [2048, 7168], P('row', 'col'), may hold values from -0.125 to 0.125
- down_weight: bfloat16 [2048, 7168], P('row', 'col'), may hold values from -0.125 to 0.125
Outputs:
- d_inputs: bfloat16 [16384, 2048], P('row', 'col')
- gate_grad: bfloat16 [2048, 7168], P('row', 'col')
- up_grad: bfloat16 [2048, 7168], P('row', 'col')
- down_grad: bfloat16 [2048, 7168], P('row', 'col')
The draws below stay inside these ranges and needn't reach their ends.
All inputs are finite; a program needn't handle non-finite values.
Results may differ from the reference program's by a relative error of at most 0.015.
Values may be sent and summed in bfloat16 or wider, within the bound.
No kernel may reach another device: no remote copies, remote signals or barrier semaphores. Data moves between devices by JAX's collectives and lax.ppermute only.
A program may use at most 128 MiB of HBM per device.

```python
import math
import jax
import jax.numpy as jnp
from jax import lax

D = 2048
FF = 7168
TOK_DEV = 512
TOKENS = 16384
N_ROW = 32


def strengthened(array, stream_key, source, target, blocks, factor):
    def block_of(axis_at):
        return (jnp.arange(array.shape[axis_at]) // (array.shape[axis_at] // blocks)).reshape((-1,) + (1,) * (array.ndim - 1 - axis_at))

    one_side = jax.random.permutation(stream_key, blocks)[block_of(target)]
    second = (block_of(target) + blocks // 2) % blocks
    return jnp.where((block_of(source) == one_side) | (block_of(source) == second), factor * array, array)


def steps_of(key, shape, split, low, largest):
    level, own = 1.0, jax.random.fold_in(key, 6)
    for axis_at, parts in split:
        draws = jnp.exp(jax.random.uniform(jax.random.fold_in(own, axis_at), (parts,), jnp.float32, low / len(split), largest / len(split)))
        level = level * jnp.repeat(draws, shape[axis_at] // parts).reshape([-1 if axis == axis_at else 1 for axis in range(len(shape))])
    return level


def normal_values(own_key, extent, scale, most, shards=(), held_as=jnp.bfloat16):
    values = scale * jax.random.normal(own_key, extent, jnp.float32)
    if shards:
        values = values * steps_of(own_key, extent, shards, -0.22, 0.18)
    return jnp.clip(values, -most, most).astype(held_as)


def noise_with(stream_key, shape, width, most, shards, heavy, kind=jnp.bfloat16):
    entries = width * jax.random.normal(stream_key, shape, jnp.float32)
    if shards:
        entries = entries * steps_of(stream_key, shape, shards, -0.22, 0.18)
    return jnp.clip(strengthened(entries, jax.random.fold_in(stream_key, 3), *heavy), -most, most).astype(kind)


def setup_inputs(seed: int = 0) -> dict:
    streams_of = jax.random.split(jax.random.key(seed), 8)
    return {
        "inputs": noise_with(streams_of[0], (TOKENS, D), 1.0, 6.0, ((0, 32), (1, 8)), (0, 1, 32, 2.75)),
        "grad_out": noise_with(streams_of[1], (TOKENS, D), 1.0, 6.0, ((0, 32), (1, 8)), (0, 1, 32, 2.75)),
        "gate_pre": normal_values(streams_of[2], (TOKENS, FF), 1.5, 8.0, ((0, 32), (1, 8))),
        "up_pre": normal_values(streams_of[3], (TOKENS, FF), 1.0, 6.0, ((0, 32), (1, 8))),
        "gate_weight": normal_values(streams_of[4], (D, FF), D ** -0.5, 0.125, ((0, 32), (1, 8))),
        "up_weight": normal_values(streams_of[5], (D, FF), D ** -0.5, 0.125, ((0, 32), (1, 8))),
        "down_weight": normal_values(streams_of[6], (D, FF), D ** -0.5, 0.125, ((0, 32), (1, 8))),
    }


def block_sums(left, right, factor):

    def step(total, index):
        start = (index * TOK_DEV).astype(jnp.int32)
        left_block = lax.dynamic_slice_in_dim(left, start, TOK_DEV, 0)
        right_block = lax.dynamic_slice_in_dim(right, start, TOK_DEV, 0)
        term = jnp.dot(left_block.T, right_block, preferred_element_type=jnp.float32) * factor
        rounded = lax.optimization_barrier(term.astype(jnp.bfloat16))
        return (total + rounded.astype(jnp.float32), None)
    total, _ = lax.scan(step, jnp.zeros((D, FF), jnp.float32), jnp.arange(N_ROW, dtype=jnp.int32))
    return total.astype(jnp.bfloat16)

def reference(inputs, grad_out, gate_pre, up_pre, gate_weight, up_weight, down_weight):
    d_hidden = jnp.dot(grad_out, down_weight, preferred_element_type=jnp.float32)
    gate_vals = gate_pre.astype(jnp.float32)
    up_vals = up_pre.astype(jnp.float32)
    sigma = jax.nn.sigmoid(gate_vals)
    active = gate_vals * sigma
    hidden = (active * up_vals).astype(jnp.bfloat16)
    d_gate = (d_hidden * up_vals * sigma * (1.0 + gate_vals * (1.0 - sigma))).astype(jnp.bfloat16)
    d_up = (d_hidden * active).astype(jnp.bfloat16)
    d_inputs = jnp.dot(d_gate, gate_weight.T, preferred_element_type=jnp.float32)
    d_inputs = d_inputs + jnp.dot(d_up, up_weight.T, preferred_element_type=jnp.float32)
    factor = 1.0 / math.sqrt(TOKENS)
    down_grad = block_sums(grad_out, hidden, factor)
    gate_grad = block_sums(inputs, d_gate, factor)
    up_grad = block_sums(inputs, d_up, factor)
    return (d_inputs.astype(jnp.bfloat16), gate_grad, up_grad, down_grad)
```

```python
import functools
import math

import jax
import jax.numpy as jnp
from jax import lax
from jax.experimental import pallas as pl
from jax.experimental.pallas import tpu as pltpu
from jax.sharding import PartitionSpec as P

Z, Y = 8, 4


def hop(value, dz, dy):
    pairs = [(z * Y + y, (z + dz) % Z * Y + (y + dy) % Y) for z in range(Z) for y in range(Y)]
    return lax.ppermute(value, "row", pairs)


def along_z(value, step):
    return hop(value, step, 0)


def along_y(value, step):
    return hop(value, 0, step)


def ring_gather(own, size, send, split):
    half = size // 2
    found = [None] * size
    found[0] = own
    up = down = own
    for step in range(1, half):
        up, down = send(up, 1), send(down, -1)
        found[size - step], found[step] = up, down
    if split:
        middle = own.shape[0] // 2
        found[half] = jnp.concatenate([send(up[:middle], 1), send(down[middle:], -1)], axis=0)
    else:
        found[half] = send(up, 1)
    return found


def ring_reduce(size, term, send, split):
    half = size // 2
    far = term(half)
    if split:
        middle = far.shape[0] // 2
        up, down = send(far[:middle].astype(jnp.bfloat16), 1), send(far[middle:].astype(jnp.bfloat16), -1)
        rest = [(0, 0, 0)] * (far.ndim - 1)
        zero = jnp.zeros((), jnp.bfloat16)
        up = lax.pad(up, zero, [(0, far.shape[0] - middle, 0)] + rest)
        down = lax.pad(down, zero, [(middle, 0, 0)] + rest)
    else:
        up, down = send(far.astype(jnp.bfloat16), 1), None
    for away in range(half - 1, 0, -1):
        up = send((term(away) + up.astype(jnp.float32)).astype(jnp.bfloat16), 1)
        left = term(size - away)
        if down is not None:
            left = left + down.astype(jnp.float32)
        down = send(left.astype(jnp.bfloat16), -1)
    return term(0) + up.astype(jnp.float32) + down.astype(jnp.float32)


def rotate_kernel(shift_ref, source_ref, *out_refs, orders, cuts):
    block = source_ref.shape[0] // (Z * Y)
    z, y = shift_ref[0], shift_ref[1]
    for q in range(Z):
        for p in range(Y):
            start = lax.rem(z + q, Z) * Y + lax.rem(y + p, Y)
            rows = source_ref[pl.ds(pl.multiple_of(start * block, block), block), :]
            for out_ref, order, (low, high) in zip(out_refs, orders, cuts):
                place = q * Y + p if order == "z" else p * Z + q
                out_ref[pl.ds(place * block, block), :] = rows[:, low:high]


def rotate(value, z, y, orders, cuts):
    rows = value.shape[0]
    shapes = [jax.ShapeDtypeStruct((rows, high - low), value.dtype) for low, high in cuts]
    return pl.pallas_call(
        functools.partial(rotate_kernel, orders=orders, cuts=cuts),
        out_shape=shapes,
        grid_spec=pltpu.PrefetchScalarGridSpec(
            num_scalar_prefetch=1,
            grid=(1,),
            in_specs=[pl.BlockSpec(value.shape, lambda i, s: (0, 0))],
            out_specs=[pl.BlockSpec(shape.shape, lambda i, s: (0, 0)) for shape in shapes],
        ),
        cost_estimate=pl.CostEstimate(
            flops=0, transcendentals=0, bytes_accessed=4 * value.size + 2 * sum(s.size for s in shapes)
        ),
        name="rotate",
    )(jnp.stack([z, y]).astype(jnp.int32), value)


def matmul(left, right, left_axis, right_axis):
    return lax.dot_general(
        left, right, (((left_axis,), (right_axis,)), ((), ())), preferred_element_type=jnp.float32
    )


def gather_rows(left, right):
    block = left.shape[0]
    stack = jnp.stack(ring_gather(left, Y, along_y, False))
    lefts = ring_gather(stack, Z, along_z, False)
    column = jnp.stack(ring_gather(right, Z, along_z, False))
    rights = ring_gather(column, Y, along_y, True)
    return (
        jnp.concatenate(lefts, axis=0).reshape(Z * Y * block, -1),
        jnp.stack(rights, axis=1).reshape(Z * Y * block, -1),
    )


def reduce_rows(by_z, by_y, left, right, factor):
    block = by_z.shape[0] // (Z * Y)

    def left_term(q):
        rows = by_z[q * Y * block : (q + 1) * Y * block]
        return (matmul(rows, left, 1, 0) * factor).reshape(Y, block, -1)

    def right_term(p):
        rows = by_y[p * Z * block : (p + 1) * Z * block]
        return (matmul(rows, right, 1, 0) * factor).reshape(Z, block, -1)

    left_sum = ring_reduce(Z, left_term, along_z, True)
    left_sum = ring_reduce(Y, lambda p: left_sum[p], along_y, False)
    right_sum = ring_reduce(Y, right_term, along_y, True)
    right_sum = ring_reduce(Z, lambda q: right_sum[q], along_z, False)
    return left_sum.astype(jnp.bfloat16), right_sum.astype(jnp.bfloat16)


def body(inputs, grad_out, gate_pre, up_pre, gate_weight, up_weight, down_weight):
    factor = 1.0 / math.sqrt(grad_out.shape[0] * Z * Y)
    tokens, hidden_here = gate_pre.shape
    row = lax.axis_index("row")
    z, y = lax.div(row, Y), lax.rem(row, Y)
    cut = hidden_here * 3 // 7
    rest = hidden_here - cut

    shared = lax.all_gather(jnp.concatenate([grad_out.T, inputs.T], axis=1), "col", axis=0, tiled=True)
    grads_z, grads_y, ins_z, ins_y = rotate(
        shared, z, y, "zyzy", [(0, tokens), (0, tokens), (tokens, 2 * tokens), (tokens, 2 * tokens)]
    )

    weights_left, weights_right = gather_rows(
        jnp.concatenate([down_weight[:, :cut], gate_weight[:, :cut], up_weight[:, :cut]], axis=1),
        jnp.concatenate([down_weight[:, cut:], gate_weight[:, cut:], up_weight[:, cut:]], axis=1),
    )

    gate_vals = gate_pre.astype(jnp.float32)
    up_vals = up_pre.astype(jnp.float32)
    sigma = jax.nn.sigmoid(gate_vals)
    active = gate_vals * sigma
    hidden = (active * up_vals).astype(jnp.bfloat16)
    down_parts = reduce_rows(grads_z, grads_y, hidden[:, :cut], hidden[:, cut:], factor)

    def half(weights, width, low, high):
        d_hidden = matmul(grads_z, weights[:, :width], 0, 0)
        g, u, s, a = (v[:, low:high] for v in (gate_vals, up_vals, sigma, active))
        d_gate = (d_hidden * u * s * (1.0 + g * (1.0 - s))).astype(jnp.bfloat16)
        d_up = (d_hidden * a).astype(jnp.bfloat16)
        return jnp.concatenate([d_gate, d_up], axis=1)

    both_left = half(weights_left, cut, 0, cut)
    both_right = half(weights_right, rest, cut, hidden_here)
    part = matmul(weights_left[:, cut:], both_left, 1, 1) + matmul(weights_right[:, rest:], both_right, 1, 1)
    (part,) = rotate(part.astype(jnp.bfloat16), Z - z, Y - y, "z", [(0, tokens)])
    d_inputs = lax.psum_scatter(part, "col", scatter_dimension=0, tiled=True).T

    left, right = reduce_rows(ins_z, ins_y, both_left, both_right, factor)
    gate_grad = jnp.concatenate([left[:, :cut], right[:, :rest]], axis=1)
    up_grad = jnp.concatenate([left[:, cut:], right[:, rest:]], axis=1)
    return (d_inputs, gate_grad, up_grad, jnp.concatenate(down_parts, axis=1))


def solution(mesh):
    spec = P("row", "col")
    return jax.shard_map(
        body, mesh=mesh, in_specs=(spec,) * 7, out_specs=(spec,) * 4, check_vma=False
    )
```

```python
import functools
import math

import jax
import jax.numpy as jnp
from jax import lax
from jax.experimental import pallas as pl
from jax.experimental.pallas import tpu as pltpu
from jax.sharding import PartitionSpec as P

Z, Y = 8, 4


def hop(value, dz, dy):
    pairs = [(z * Y + y, (z + dz) % Z * Y + (y + dy) % Y) for z in range(Z) for y in range(Y)]
    return lax.ppermute(value, "row", pairs)


def along_z(value, step):
    return hop(value, step, 0)


def along_y(value, step):
    return hop(value, 0, step)


def ring_gather(own, size, send, split):
    half = size // 2
    found = [None] * size
    found[0] = own
    up = down = own
    for step in range(1, half):
        up, down = send(up, 1), send(down, -1)
        found[size - step], found[step] = up, down
    if split:
        middle = own.shape[0] // 2
        found[half] = jnp.concatenate([send(up[:middle], 1), send(down[middle:], -1)], axis=0)
    else:
        found[half] = send(up, 1)
    return found


def wide(value):
    return value.astype(jnp.float32)


def ring_reduce(terms, send, split):
    size = terms.shape[0]
    half = size // 2
    far = terms[half].astype(jnp.bfloat16)
    if split:
        middle = far.shape[0] // 2
        up, down = send(far[:middle], 1), send(far[middle:], -1)
        rest = [(0, 0, 0)] * (far.ndim - 1)
        zero = jnp.zeros((), jnp.bfloat16)
        up = lax.pad(up, zero, [(0, far.shape[0] - middle, 0)] + rest)
        down = lax.pad(down, zero, [(middle, 0, 0)] + rest)
    else:
        up, down = send(far, 1), None
    for away in range(half - 1, 0, -1):
        up = send((wide(terms[away]) + wide(up)).astype(jnp.bfloat16), 1)
        left = wide(terms[size - away])
        if down is not None:
            left = left + wide(down)
        down = send(left.astype(jnp.bfloat16), -1)
    return wide(terms[0]) + wide(up) + wide(down)


def rotate_kernel(shift_ref, source_ref, *out_refs, orders, cuts):
    block = source_ref.shape[0] // (Z * Y)
    z, y = shift_ref[0], shift_ref[1]

    def move(index, carry):
        q, p = lax.div(index, Y), lax.rem(index, Y)
        start = lax.rem(z + q, Z) * Y + lax.rem(y + p, Y)
        rows = source_ref[pl.ds(pl.multiple_of(start * block, block), block), :]
        for out_ref, order, (low, high) in zip(out_refs, orders, cuts):
            place = index if order == "z" else p * Z + q
            out_ref[pl.ds(pl.multiple_of(place * block, block), block), :] = rows[:, low:high]
        return carry

    lax.fori_loop(0, Z * Y, move, 0)


def rotate(value, z, y, orders, cuts):
    rows = value.shape[0]
    shapes = [jax.ShapeDtypeStruct((rows, high - low), value.dtype) for low, high in cuts]
    return pl.pallas_call(
        functools.partial(rotate_kernel, orders=orders, cuts=cuts),
        out_shape=shapes,
        grid_spec=pltpu.PrefetchScalarGridSpec(
            num_scalar_prefetch=1,
            grid=(1,),
            in_specs=[pl.BlockSpec(value.shape, lambda i, s: (0, 0))],
            out_specs=[pl.BlockSpec(shape.shape, lambda i, s: (0, 0)) for shape in shapes],
        ),
        cost_estimate=pl.CostEstimate(
            flops=0, transcendentals=0, bytes_accessed=4 * value.size + 2 * sum(s.size for s in shapes)
        ),
        name="rotate",
    )(jnp.stack([z, y]).astype(jnp.int32), value)


def matmul(left, right, left_axis, right_axis):
    return lax.dot_general(
        left, right, (((left_axis,), (right_axis,)), ((), ())), preferred_element_type=jnp.float32
    )


def gather_rows(left, right):
    block = left.shape[0]
    stack = jnp.stack(ring_gather(left, Y, along_y, False))
    column = jnp.stack(ring_gather(right, Z, along_z, False))
    stack, column = lax.optimization_barrier((stack, column))
    lefts = ring_gather(stack, Z, along_z, False)
    rights = ring_gather(column, Y, along_y, True)
    return (
        jnp.concatenate(lefts, axis=0).reshape(Z * Y * block, -1),
        jnp.stack(rights, axis=1).reshape(Z * Y * block, -1),
    )


def long_rings(by_z, by_y, left, right, factor):
    block = by_z.shape[0] // (Z * Y)
    left = (matmul(by_z, left, 1, 0) * factor).astype(jnp.bfloat16)
    right = (matmul(by_y, right, 1, 0) * factor).astype(jnp.bfloat16)
    return (
        ring_reduce(left.reshape(Z, Y, block, -1), along_z, True),
        ring_reduce(right.reshape(Y, Z, block, -1), along_y, True),
    )


def body(inputs, grad_out, gate_pre, up_pre, gate_weight, up_weight, down_weight):
    factor = 1.0 / math.sqrt(grad_out.shape[0] * Z * Y)
    tokens, hidden_here = gate_pre.shape
    row = lax.axis_index("row")
    z, y = lax.div(row, Y), lax.rem(row, Y)
    cut = hidden_here * 3 // 7
    rest = hidden_here - cut

    shared = lax.all_gather(jnp.concatenate([grad_out.T, inputs.T], axis=1), "col", axis=0, tiled=True)
    grads_z, grads_y, ins_z, ins_y = rotate(
        shared, z, y, "zyzy", [(0, tokens), (0, tokens), (tokens, 2 * tokens), (tokens, 2 * tokens)]
    )

    weights_left, weights_right = gather_rows(
        jnp.concatenate([down_weight[:, :cut], gate_weight[:, :cut], up_weight[:, :cut]], axis=1),
        jnp.concatenate([down_weight[:, cut:], gate_weight[:, cut:], up_weight[:, cut:]], axis=1),
    )

    gate_vals = gate_pre.astype(jnp.float32)
    up_vals = up_pre.astype(jnp.float32)
    sigma = jax.nn.sigmoid(gate_vals)
    active = gate_vals * sigma
    hidden = (active * up_vals).astype(jnp.bfloat16)
    down_sums = long_rings(grads_z, grads_y, hidden[:, :cut], hidden[:, cut:], factor)

    def half(weights, width, low, high):
        d_hidden = matmul(grads_z, weights[:, :width], 0, 0)
        g, u, s, a = (v[:, low:high] for v in (gate_vals, up_vals, sigma, active))
        d_gate = (d_hidden * u * s * (1.0 + g * (1.0 - s))).astype(jnp.bfloat16)
        d_up = (d_hidden * a).astype(jnp.bfloat16)
        return jnp.concatenate([d_gate, d_up], axis=1)

    both_left = half(weights_left, cut, 0, cut)
    both_right = half(weights_right, rest, cut, hidden_here)
    part = matmul(weights_left[:, cut:], both_left, 1, 1) + matmul(weights_right[:, rest:], both_right, 1, 1)
    (part,) = rotate(part.astype(jnp.bfloat16), Z - z, Y - y, "z", [(0, tokens)])
    d_inputs = lax.psum_scatter(part, "col", scatter_dimension=0, tiled=True).T

    both_sums = long_rings(ins_z, ins_y, both_left, both_right, factor)
    left, right = (jnp.concatenate(pair, axis=2) for pair in zip(down_sums, both_sums))
    left = ring_reduce(left, along_y, False).astype(jnp.bfloat16)
    right = ring_reduce(right, along_z, False).astype(jnp.bfloat16)
    down_grad, gate_grad, up_grad = (
        jnp.concatenate([left[:, i * cut : (i + 1) * cut], right[:, i * rest : (i + 1) * rest]], axis=1)
        for i in range(3)
    )
    return (d_inputs, gate_grad, up_grad, down_grad)


def solution(mesh):
    spec = P("row", "col")
    return jax.shard_map(
        body, mesh=mesh, in_specs=(spec,) * 7, out_specs=(spec,) * 4, check_vma=False
    )
```

```python
import functools
import math

import jax
import jax.numpy as jnp
from jax import lax
from jax.experimental import pallas as pl
from jax.experimental.pallas import tpu as pltpu
from jax.sharding import PartitionSpec as P

Z, Y = 8, 4


def wide(value):
    return value.astype(jnp.float32)


def narrow(value):
    return value.astype(jnp.bfloat16)


def matmul(left, right, left_axis, right_axis):
    return lax.dot_general(
        left, right, (((left_axis,), (right_axis,)), ((), ())), preferred_element_type=jnp.float32
    )


def along_z(value, step):
    pairs = [(z * Y + y, (z + step) % Z * Y + y) for z in range(Z) for y in range(Y)]
    return lax.ppermute(value, "row", pairs)


def swap_cores(value):
    size = lax.axis_size("col")
    return lax.ppermute(value, "col", [(i, i ^ 1) for i in range(size)])


def partners(axis, second):
    def send(value):
        size = lax.axis_size("col")
        pairs = []
        for row in range(Z * Y):
            for col in range(size):
                mask = 3 if (col & 1) != second else 1
                if axis == "y":
                    target = (row ^ mask) * size + col
                else:
                    target = row * size + (col ^ (2 * mask))
                pairs.append((row * size + col, target))
        return lax.ppermute(value, ("row", "col"), pairs)

    return send


def place_of(entry, core):
    odd = 1 + 2 * lax.bitwise_xor(lax.rem(entry + 1, 2), core)
    return jnp.where(entry == 0, 0, jnp.where(entry == 3, 2, odd))


def entry_of(mask, core):
    odd = 1 + lax.bitwise_xor(lax.div(mask, 2), core)
    return jnp.where(mask == 0, 0, jnp.where(mask == 2, 3, odd))


def four_gather(own, axis):
    first = partners(axis, 0)(own)
    pair = partners(axis, 1)(jnp.stack([own, first]))
    return [own, first, pair[0], pair[1]]


def four_reduce(terms, axis):
    got = partners(axis, 1)(narrow(terms[2:]))
    last = partners(axis, 0)(narrow(wide(terms[1]) + wide(got[1])))
    return wide(terms[0]) + wide(got[0]) + wide(last)


def ring_gather(own, split):
    half, rows = Z // 2, own.shape[0]
    found = [(0, 0, own)]
    up = down = own
    for step in range(1, half):
        up, down = along_z(up, 1), along_z(down, -1)
        found += [(Z - step, 0, up), (step, 0, down)]
    if split:
        middle = rows // 2
        return found + [(half, 0, along_z(up[:middle], 1)), (half, middle, along_z(down[middle:], -1))]
    return found + [(half, 0, along_z(up, 1))]


def ring_reduce(terms, split):
    half = Z // 2
    far = narrow(terms[half])
    if split:
        middle = far.shape[0] // 2
        up, down = along_z(far[:middle], 1), along_z(far[middle:], -1)
        rest = [(0, 0, 0)] * (far.ndim - 1)
        zero = jnp.zeros((), jnp.bfloat16)
        up = lax.pad(up, zero, [(0, far.shape[0] - middle, 0)] + rest)
        down = lax.pad(down, zero, [(middle, 0, 0)] + rest)
    else:
        up, down = along_z(far, 1), None
    for away in range(half - 1, 0, -1):
        up = along_z(narrow(wide(terms[away]) + wide(up)), 1)
        left = wide(terms[Z - away])
        if down is not None:
            left = left + wide(down)
        down = along_z(narrow(left), -1)
    return wide(terms[0]) + wide(up) + wide(down)


def turn_in_kernel(place_ref, mine_ref, theirs_ref, grads_z, grads_y, ins_z, ins_y, *, block, tokens):
    z, y, x, core = (place_ref[i] for i in range(4))

    def move(index, carry):
        q, p = lax.div(index, Y), lax.rem(index, Y)
        far_z = lax.rem(z + q, Z)
        far_y = lax.bitwise_xor(y, place_of(p, core))
        far_x, far_core = lax.div(far_z, 2), lax.rem(far_z, 2)
        start = (entry_of(lax.bitwise_xor(far_x, x), far_core) * Y + far_y) * block
        start = pl.multiple_of(start, block)
        by_z = pl.ds(pl.multiple_of(index * block, block), block)
        by_y = pl.ds(pl.multiple_of((p * Z + q) * block, block), block)

        def store(source_ref):
            rows = source_ref[pl.ds(start, block), :]
            grads_z[by_z, :] = rows[:, :tokens]
            grads_y[by_y, :] = rows[:, :tokens]
            ins_z[by_z, :] = rows[:, tokens:]
            ins_y[by_y, :] = rows[:, tokens:]

        @pl.when(far_core == core)
        def _():
            store(mine_ref)

        @pl.when(far_core != core)
        def _():
            store(theirs_ref)

        return carry

    lax.fori_loop(0, Z * Y, move, 0)


def turn_back_kernel(place_ref, left_ref, right_ref, out_ref, *, block):
    z, y, x, core = (place_ref[i] for i in range(4))

    def move(index, carry):
        other, rest = lax.div(index, 16), lax.rem(index, 16)
        entry, far_y = lax.div(rest, Y), lax.rem(rest, Y)
        far_core = lax.bitwise_xor(core, other)
        far_z = 2 * lax.bitwise_xor(x, place_of(entry, far_core)) + far_core
        q = lax.rem(far_z - z + Z, Z)
        p = entry_of(lax.bitwise_xor(far_y, y), core)
        left = left_ref[pl.ds(pl.multiple_of((q * Y + p) * block, block), block), :]
        right = right_ref[pl.ds(pl.multiple_of((p * Z + q) * block, block), block), :]
        out_ref[pl.ds(pl.multiple_of(index * block, block), block), :] = narrow(left + right)
        return carry

    lax.fori_loop(0, Z * Y, move, 0)


def local(kernel, name, place, operands, shapes):
    return pl.pallas_call(
        kernel,
        out_shape=shapes,
        grid_spec=pltpu.PrefetchScalarGridSpec(
            num_scalar_prefetch=1,
            grid=(1,),
            in_specs=[pl.BlockSpec(value.shape, lambda i, s: (0, 0)) for value in operands],
            out_specs=[pl.BlockSpec(shape.shape, lambda i, s: (0, 0)) for shape in shapes],
        ),
        cost_estimate=pl.CostEstimate(
            flops=0,
            transcendentals=0,
            bytes_accessed=sum(v.size * v.dtype.itemsize for v in [*operands, *shapes]),
        ),
        name=name,
    )(place, *operands)


def gradient_terms(features, values, factor, size):
    rows = features.shape[0]
    terms = narrow(matmul(features, values, 1, 0) * factor)
    return terms.reshape(size, Z * Y // size, rows // (Z * Y), -1)


def body(inputs, grad_out, gate_pre, up_pre, gate_weight, up_weight, down_weight):
    factor = 1.0 / math.sqrt(grad_out.shape[0] * Z * Y)
    tokens, width = gate_pre.shape
    block = down_weight.shape[0]
    rows = Z * Y * block
    row, col = lax.axis_index("row"), lax.axis_index("col")
    place = jnp.stack([lax.div(row, Y), lax.rem(row, Y), lax.div(col, 2), lax.rem(col, 2)])
    place = place.astype(jnp.int32)
    unit = width // 7

    mine = jnp.concatenate(four_gather(jnp.concatenate([grad_out.T, inputs.T], axis=1), "x"), axis=0)

    lead, trail = down_weight, up_weight
    lead = jnp.concatenate([lead, gate_weight[:, : 2 * unit]], axis=1)
    trail = jnp.concatenate([gate_weight[:, 2 * unit :], trail], axis=1)
    stack = jnp.stack(four_gather(lead, "y"))
    column = [None] * Z
    for q, _, piece in ring_gather(trail, False):
        column[q] = piece
    stack, column = lax.optimization_barrier((stack, jnp.stack(column)))
    lead_pieces = ring_gather(stack, True)
    trail_all = jnp.concatenate(four_gather(column, "y"), axis=0).reshape(rows, -1)

    shape = jax.ShapeDtypeStruct((rows, tokens), jnp.bfloat16)
    grads_z, grads_y, ins_z, ins_y = local(
        functools.partial(turn_in_kernel, block=block, tokens=tokens),
        "turn_in", place, [mine, swap_cores(mine)], [shape] * 4,
    )

    gate_early, up_early = wide(gate_pre), wide(up_pre)
    hidden = narrow(gate_early * jax.nn.sigmoid(gate_early) * up_early)
    down_left = ring_reduce(gradient_terms(grads_z, hidden[:, : 3 * unit], factor, Z), True)
    down_right = four_reduce(gradient_terms(grads_y, hidden[:, 3 * unit :], factor, Y), "y")

    d_hidden = None
    lead_gate = [None] * len(lead_pieces)
    for i, (q, first, piece) in enumerate(sorted(lead_pieces, key=lambda found: found[:2])):
        piece = piece.reshape(-1, piece.shape[-1])
        start = (q * Y + first) * block
        product = matmul(grads_z[start : start + piece.shape[0]], piece[:, :width], 0, 0)
        d_hidden = product if d_hidden is None else d_hidden + product
        lead_gate[i] = piece[:, width:]
    lead_gate = jnp.concatenate(lead_gate, axis=0)

    gate_late, up_late = lax.optimization_barrier((gate_pre, up_pre, hidden))[:2]
    gate_late, up_late = wide(gate_late), wide(up_late)
    sigma = jax.nn.sigmoid(gate_late)
    d_gate = narrow(d_hidden * up_late * sigma * (1.0 + gate_late * (1.0 - sigma)))
    d_up = narrow(d_hidden * (gate_late * sigma))

    both_left = gradient_terms(ins_z, d_gate[:, : 6 * unit], factor, Z)
    both_right = jnp.concatenate([d_gate[:, 6 * unit :], d_up], axis=1)
    both_right = gradient_terms(ins_y, both_right, factor, Y)
    both_left = ring_reduce(both_left, True)
    both_right = four_reduce(both_right, "y")

    part_left = matmul(lead_gate, d_gate[:, : 2 * unit], 1, 1)
    part_right = matmul(trail_all, jnp.concatenate([d_gate[:, 2 * unit :], d_up], axis=1), 1, 1)
    (part,) = local(
        functools.partial(turn_back_kernel, block=block),
        "turn_back", place, [part_left, part_right], [shape],
    )
    part = part.reshape(2, 4, Y * block, tokens)
    part = wide(part[0]) + wide(swap_cores(part[1]))
    d_inputs = narrow(four_reduce(part, "x")).T

    left = jnp.concatenate([down_left, both_left], axis=2)
    right = jnp.concatenate([down_right, both_right], axis=2)
    left = narrow(four_reduce(left, "y"))
    right = narrow(ring_reduce(right, False))
    cut = 4 * unit
    down_grad = jnp.concatenate([left[:, : 3 * unit], right[:, :cut]], axis=1)
    gate_grad = jnp.concatenate([left[:, 3 * unit :], right[:, cut : cut + unit]], axis=1)
    return (d_inputs, gate_grad, right[:, cut + unit :], down_grad)


def solution(mesh):
    spec = P("row", "col")
    return jax.shard_map(
        body, mesh=mesh, in_specs=(spec,) * 7, out_specs=(spec,) * 4, check_vma=False
    )
```

```python
import functools
import math

import jax
import jax.numpy as jnp
from jax import lax
from jax.experimental import pallas as pl
from jax.experimental.pallas import tpu as pltpu
from jax.sharding import PartitionSpec as P


Z, Y = 8, 4


def wide(value):
    return value.astype(jnp.float32)


def narrow(value):
    return value.astype(jnp.bfloat16)


def matmul(left, right, left_axis, right_axis):
    return lax.dot_general(
        left, right, (((left_axis,), (right_axis,)), ((), ())), preferred_element_type=jnp.float32
    )


def along_z(value, step):
    pairs = [(z * Y + y, (z + step) % Z * Y + y) for z in range(Z) for y in range(Y)]
    return lax.ppermute(value, "row", pairs)


def swap_cores(value):
    size = lax.axis_size("col")
    return lax.ppermute(value, "col", [(i, i ^ 1) for i in range(size)])


def partners(axis, second):
    def send(value):
        size = lax.axis_size("col")
        pairs = []
        for row in range(Z * Y):
            for col in range(size):
                mask = 3 if (col & 1) != second else 1
                if axis == "y":
                    target = (row ^ mask) * size + col
                else:
                    target = row * size + (col ^ (2 * mask))
                pairs.append((row * size + col, target))
        return lax.ppermute(value, ("row", "col"), pairs)

    return send


def place_of(entry, core):
    odd = 1 + 2 * lax.bitwise_xor(lax.rem(entry + 1, 2), core)
    return jnp.where(entry == 0, 0, jnp.where(entry == 3, 2, odd))


def entry_of(mask, core):
    odd = 1 + lax.bitwise_xor(lax.div(mask, 2), core)
    return jnp.where(mask == 0, 0, jnp.where(mask == 2, 3, odd))


def four_gather(own, axis):
    first = partners(axis, 0)(own)
    pair = partners(axis, 1)(jnp.stack([own, first]))
    return [own, first, pair[0], pair[1]]


def four_reduce(terms, axis):
    got = partners(axis, 1)(narrow(terms[2:]))
    last = partners(axis, 0)(narrow(wide(terms[1]) + wide(got[1])))
    return wide(terms[0]) + wide(got[0]) + wide(last)


def ring_gather(own, split, gate=None):
    half, rows = Z // 2, own.shape[0]
    found = [(0, 0, own)]
    up = down = own
    for step in range(1, half):
        up, down = along_z(up, 1), along_z(down, -1)
        if step == 1 and gate is not None:
            up, down, gate = lax.optimization_barrier((up, down, gate))
        found += [(Z - step, 0, up), (step, 0, down)]
    if split:
        middle = rows // 2
        up, down = along_z(up[:middle], 1), along_z(down[middle:], -1)
        found += [(half, 0, up), (half, middle, down)]
    else:
        found += [(half, 0, along_z(up, 1))]
    return found, gate


def ring_reduce(terms, split):
    half = Z // 2
    far = narrow(terms[half])
    if split:
        middle = far.shape[0] // 2
        up, down = along_z(far[:middle], 1), along_z(far[middle:], -1)
        rest = [(0, 0, 0)] * (far.ndim - 1)
        zero = jnp.zeros((), jnp.bfloat16)
        up = lax.pad(up, zero, [(0, far.shape[0] - middle, 0)] + rest)
        down = lax.pad(down, zero, [(middle, 0, 0)] + rest)
    else:
        up, down = along_z(far, 1), None
    for away in range(half - 1, 0, -1):
        up = along_z(narrow(wide(terms[away]) + wide(up)), 1)
        left = wide(terms[Z - away])
        if down is not None:
            left = left + wide(down)
        down = along_z(narrow(left), -1)
    return wide(terms[0]) + wide(up) + wide(down)


def turn_in_kernel(place_ref, mine_ref, theirs_ref, grads_z, grads_y, ins_z, ins_y, *, block, tokens):
    z, y, x, core = (place_ref[i] for i in range(4))

    def move(index, carry):
        q, p = lax.div(index, Y), lax.rem(index, Y)
        far_z = lax.rem(z + q, Z)
        far_y = lax.bitwise_xor(y, place_of(p, core))
        far_x, far_core = lax.div(far_z, 2), lax.rem(far_z, 2)
        start = (entry_of(lax.bitwise_xor(far_x, x), far_core) * Y + far_y) * block
        start = pl.multiple_of(start, block)
        by_z = pl.ds(pl.multiple_of(index * block, block), block)
        by_y = pl.ds(pl.multiple_of((p * Z + q) * block, block), block)

        def store(source_ref):
            rows = source_ref[pl.ds(start, block), :]
            grads_z[by_z, :] = rows[:, :tokens]
            grads_y[by_y, :] = rows[:, :tokens]
            ins_z[by_z, :] = rows[:, tokens:]
            ins_y[by_y, :] = rows[:, tokens:]

        @pl.when(far_core == core)
        def _():
            store(mine_ref)

        @pl.when(far_core != core)
        def _():
            store(theirs_ref)

        return carry

    lax.fori_loop(0, Z * Y, move, 0)


def turn_back_kernel(place_ref, left_ref, right_ref, out_ref, *, block):
    z, y, x, core = (place_ref[i] for i in range(4))

    def move(index, carry):
        other, rest = lax.div(index, 16), lax.rem(index, 16)
        entry, far_y = lax.div(rest, Y), lax.rem(rest, Y)
        far_core = lax.bitwise_xor(core, other)
        far_z = 2 * lax.bitwise_xor(x, place_of(entry, far_core)) + far_core
        q = lax.rem(far_z - z + Z, Z)
        p = entry_of(lax.bitwise_xor(far_y, y), core)
        left = left_ref[pl.ds(pl.multiple_of((q * Y + p) * block, block), block), :]
        right = right_ref[pl.ds(pl.multiple_of((p * Z + q) * block, block), block), :]
        out_ref[pl.ds(pl.multiple_of(index * block, block), block), :] = narrow(left + right)
        return carry

    lax.fori_loop(0, Z * Y, move, 0)


def local_call(kernel, place, operands, shapes):
    return pl.pallas_call(
        kernel,
        out_shape=shapes,
        grid_spec=pltpu.PrefetchScalarGridSpec(
            num_scalar_prefetch=1,
            grid=(1,),
            in_specs=[pl.BlockSpec(value.shape, lambda i, s: (0, 0)) for value in operands],
            out_specs=[pl.BlockSpec(shape.shape, lambda i, s: (0, 0)) for shape in shapes],
        ),
        cost_estimate=pl.CostEstimate(
            flops=0,
            transcendentals=0,
            bytes_accessed=sum(v.size * v.dtype.itemsize for v in [*operands, *shapes]),
        ),
    )(place, *operands)


def gradient_terms(features, values, factor, size):
    rows = features.shape[0]
    terms = narrow(matmul(features, values, 1, 0) * factor)
    return terms.reshape(size, Z * Y // size, rows // (Z * Y), -1)


def body(inputs, grad_out, gate_pre, up_pre, gate_weight, up_weight, down_weight):
    factor = 1.0 / math.sqrt(grad_out.shape[0] * Z * Y)
    tokens, width = gate_pre.shape
    block = down_weight.shape[0]
    rows = Z * Y * block
    row, col = lax.axis_index("row"), lax.axis_index("col")
    place = jnp.stack([lax.div(row, Y), lax.rem(row, Y), lax.div(col, 2), lax.rem(col, 2)])
    place = place.astype(jnp.int32)
    unit = width // 7

    acts = jnp.concatenate([grad_out.T, inputs.T], axis=1)

    lead = jnp.concatenate([down_weight, gate_weight[:, : 2 * unit]], axis=1)
    trail = jnp.concatenate([gate_weight[:, 2 * unit :], up_weight], axis=1)
    mine = jnp.concatenate(four_gather(acts, "x"), axis=0)
    stack = jnp.stack(four_gather(lead, "y"))
    column = [None] * Z
    for q, _, piece in ring_gather(trail, False)[0]:
        column[q] = piece
    theirs = swap_cores(mine)
    stack, column, mine, theirs = lax.optimization_barrier((stack, jnp.stack(column), mine, theirs))

    shape = jax.ShapeDtypeStruct((rows, tokens), jnp.bfloat16)
    grads_z, grads_y, ins_z, ins_y = local_call(
        functools.partial(turn_in_kernel, block=block, tokens=tokens),
        place, [mine, theirs], [shape] * 4,
    )
    gate_early, up_early = wide(gate_pre), wide(up_pre)
    hidden = narrow(gate_early * jax.nn.sigmoid(gate_early) * up_early)
    down_left = gradient_terms(grads_z, hidden[:, : 3 * unit], factor, Z)
    down_right = gradient_terms(grads_y, hidden[:, 3 * unit :], factor, Y)
    lead_pieces, (down_left, down_right) = ring_gather(stack, True, (down_left, down_right))
    trail_all = jnp.concatenate(four_gather(column, "y"), axis=0).reshape(rows, -1)
    down_left = ring_reduce(down_left, True)
    down_right = four_reduce(down_right, "y")

    d_hidden = None
    lead_gate = [None] * len(lead_pieces)
    for i, (q, first, piece) in enumerate(sorted(lead_pieces, key=lambda found: found[:2])):
        piece = piece.reshape(-1, piece.shape[-1])
        start = (q * Y + first) * block
        product = matmul(grads_z[start : start + piece.shape[0]], piece[:, :width], 0, 0)
        d_hidden = product if d_hidden is None else d_hidden + product
        lead_gate[i] = piece[:, width:]
    lead_gate = jnp.concatenate(lead_gate, axis=0)

    gate_late, up_late = lax.optimization_barrier((gate_pre, up_pre, hidden))[:2]
    gate_late, up_late = wide(gate_late), wide(up_late)
    sigma = jax.nn.sigmoid(gate_late)
    d_gate = narrow(d_hidden * up_late * sigma * (1.0 + gate_late * (1.0 - sigma)))
    d_up = narrow(d_hidden * (gate_late * sigma))

    both_left = gradient_terms(ins_z, d_gate[:, : 6 * unit], factor, Z)
    both_right = jnp.concatenate([d_gate[:, 6 * unit :], d_up], axis=1)
    both_right = gradient_terms(ins_y, both_right, factor, Y)
    both_left = ring_reduce(both_left, True)
    both_right = four_reduce(both_right, "y")

    part_left = matmul(lead_gate, d_gate[:, : 2 * unit], 1, 1)
    part_right = matmul(trail_all, jnp.concatenate([d_gate[:, 2 * unit :], d_up], axis=1), 1, 1)
    (part,) = local_call(
        functools.partial(turn_back_kernel, block=block),
        place, [part_left, part_right], [shape],
    )
    part = part.reshape(2, 4, Y * block, tokens)
    part = wide(part[0]) + wide(swap_cores(part[1]))
    d_inputs = narrow(four_reduce(part, "x")).T

    left = jnp.concatenate([down_left, both_left], axis=2)
    right = jnp.concatenate([down_right, both_right], axis=2)
    left = narrow(four_reduce(left, "y"))
    right = narrow(ring_reduce(right, False))
    cut = 4 * unit
    down_grad = jnp.concatenate([left[:, : 3 * unit], right[:, :cut]], axis=1)
    gate_grad = jnp.concatenate([left[:, 3 * unit :], right[:, cut : cut + unit]], axis=1)
    return (d_inputs, gate_grad, right[:, cut + unit :], down_grad)


def solution(mesh):
    spec = P("row", "col")
    return jax.shard_map(body, mesh=mesh, in_specs=(spec,) * 7, out_specs=(spec,) * 4, check_vma=False)
```

```python
import functools
import math

import jax
import jax.numpy as jnp
from jax import lax
from jax.experimental import pallas as pl
from jax.experimental.pallas import tpu as pltpu
from jax.sharding import PartitionSpec as P

Z, Y = 8, 4


def hop(value, dz, dy):
    pairs = [(z * Y + y, (z + dz) % Z * Y + (y + dy) % Y) for z in range(Z) for y in range(Y)]
    return lax.ppermute(value, "row", pairs)


def along_z(value, step):
    return hop(value, step, 0)


def along_y(value, step):
    return hop(value, 0, step)


def ring_gather(own, size, send, split):
    half = size // 2
    found = [None] * size
    found[0] = own
    up = down = own
    for step in range(1, half):
        up, down = send(up, 1), send(down, -1)
        found[size - step], found[step] = up, down
    if split:
        middle = own.shape[0] // 2
        found[half] = jnp.concatenate([send(up[:middle], 1), send(down[middle:], -1)], axis=0)
    else:
        found[half] = send(up, 1)
    return found


def wide(value):
    return value.astype(jnp.float32)


def ring_reduce(terms, send, split):
    size = terms.shape[0]
    half = size // 2
    far = terms[half].astype(jnp.bfloat16)
    if split:
        middle = far.shape[0] // 2
        up, down = send(far[:middle], 1), send(far[middle:], -1)
        rest = [(0, 0, 0)] * (far.ndim - 1)
        zero = jnp.zeros((), jnp.bfloat16)
        up = lax.pad(up, zero, [(0, far.shape[0] - middle, 0)] + rest)
        down = lax.pad(down, zero, [(middle, 0, 0)] + rest)
    else:
        up, down = send(far, 1), None
    for away in range(half - 1, 0, -1):
        up = send((wide(terms[away]) + wide(up)).astype(jnp.bfloat16), 1)
        left = wide(terms[size - away])
        if down is not None:
            left = left + wide(down)
        down = send(left.astype(jnp.bfloat16), -1)
    return wide(terms[0]) + wide(up) + wide(down)


def rotate_kernel(shift_ref, source_ref, *out_refs, orders, cuts):
    block = source_ref.shape[0] // (Z * Y)
    z, y = shift_ref[0], shift_ref[1]

    def move(index, carry):
        q, p = lax.div(index, Y), lax.rem(index, Y)
        start = lax.rem(z + q, Z) * Y + lax.rem(y + p, Y)
        rows = source_ref[pl.ds(pl.multiple_of(start * block, block), block), :]
        for out_ref, order, (low, high) in zip(out_refs, orders, cuts):
            place = index if order == "z" else p * Z + q
            out_ref[pl.ds(pl.multiple_of(place * block, block), block), :] = rows[:, low:high]
        return carry

    lax.fori_loop(0, Z * Y, move, 0)


def rotate(value, z, y, orders, cuts):
    rows = value.shape[0]
    shapes = [jax.ShapeDtypeStruct((rows, high - low), value.dtype) for low, high in cuts]
    return pl.pallas_call(
        functools.partial(rotate_kernel, orders=orders, cuts=cuts),
        out_shape=shapes,
        grid_spec=pltpu.PrefetchScalarGridSpec(
            num_scalar_prefetch=1,
            grid=(1,),
            in_specs=[pl.BlockSpec(value.shape, lambda i, s: (0, 0))],
            out_specs=[pl.BlockSpec(shape.shape, lambda i, s: (0, 0)) for shape in shapes],
        ),
        cost_estimate=pl.CostEstimate(
            flops=0, transcendentals=0, bytes_accessed=4 * value.size + 2 * sum(s.size for s in shapes)
        ),
        name="rotate",
    )(jnp.stack([z, y]).astype(jnp.int32), value)


def matmul(left, right, left_axis, right_axis):
    return lax.dot_general(
        left, right, (((left_axis,), (right_axis,)), ((), ())), preferred_element_type=jnp.float32
    )


def gather_rows(left, right, later):
    block = left.shape[0]
    stack = jnp.stack(ring_gather(left, Y, along_y, False))
    column = jnp.stack(ring_gather(right, Z, along_z, False))
    stack, column, later = lax.optimization_barrier((stack, column, later))
    lefts = ring_gather(stack, Z, along_z, False)
    rights = ring_gather(column, Y, along_y, True)
    return (
        jnp.concatenate(lefts, axis=0).reshape(Z * Y * block, -1),
        jnp.stack(rights, axis=1).reshape(Z * Y * block, -1),
        later,
    )


def long_rings(by_z, by_y, left, right, factor):
    block = by_z.shape[0] // (Z * Y)
    left = (matmul(by_z, left, 1, 0) * factor).astype(jnp.bfloat16)
    right = (matmul(by_y, right, 1, 0) * factor).astype(jnp.bfloat16)
    return (
        ring_reduce(left.reshape(Z, Y, block, -1), along_z, True),
        ring_reduce(right.reshape(Y, Z, block, -1), along_y, True),
    )


def body(inputs, grad_out, gate_pre, up_pre, gate_weight, up_weight, down_weight):
    factor = 1.0 / math.sqrt(grad_out.shape[0] * Z * Y)
    tokens, hidden_here = gate_pre.shape
    row = lax.axis_index("row")
    z, y = lax.div(row, Y), lax.rem(row, Y)
    cut = hidden_here * 3 // 7
    rest = hidden_here - cut

    shared = lax.all_gather(jnp.concatenate([grad_out.T, inputs.T], axis=1), "col", axis=0, tiled=True)
    grads_z, grads_y, ins_z, ins_y = rotate(
        shared, z, y, "zyzy", [(0, tokens), (0, tokens), (tokens, 2 * tokens), (tokens, 2 * tokens)]
    )

    weights_left, weights_right, (gate_pre, up_pre) = gather_rows(
        jnp.concatenate([down_weight[:, :cut], gate_weight[:, :cut], up_weight[:, :cut]], axis=1),
        jnp.concatenate([down_weight[:, cut:], gate_weight[:, cut:], up_weight[:, cut:]], axis=1),
        (gate_pre, up_pre),
    )

    gate_early, up_early = wide(gate_pre), wide(up_pre)
    hidden = (gate_early * jax.nn.sigmoid(gate_early) * up_early).astype(jnp.bfloat16)
    gate_pre, up_pre, hidden = lax.optimization_barrier((gate_pre, up_pre, hidden))
    down_sums = long_rings(grads_z, grads_y, hidden[:, :cut], hidden[:, cut:], factor)

    def half(weights, width, low, high):
        d_hidden = matmul(grads_z, weights[:, :width], 0, 0)
        g, u = wide(gate_pre[:, low:high]), wide(up_pre[:, low:high])
        s = jax.nn.sigmoid(g)
        d_gate = (d_hidden * u * s * (1.0 + g * (1.0 - s))).astype(jnp.bfloat16)
        d_up = (d_hidden * (g * s)).astype(jnp.bfloat16)
        return jnp.concatenate([d_gate, d_up], axis=1)

    both_left = half(weights_left, cut, 0, cut)
    both_right = half(weights_right, rest, cut, hidden_here)
    part = matmul(weights_left[:, cut:], both_left, 1, 1) + matmul(weights_right[:, rest:], both_right, 1, 1)
    (part,) = rotate(part.astype(jnp.bfloat16), Z - z, Y - y, "z", [(0, tokens)])
    d_inputs = lax.psum_scatter(part, "col", scatter_dimension=0, tiled=True).T

    both_sums = long_rings(ins_z, ins_y, both_left, both_right, factor)
    left, right = (jnp.concatenate(pair, axis=2) for pair in zip(down_sums, both_sums))
    left = ring_reduce(left, along_y, False).astype(jnp.bfloat16)
    right = ring_reduce(right, along_z, False).astype(jnp.bfloat16)
    down_grad, gate_grad, up_grad = (
        jnp.concatenate([left[:, i * cut : (i + 1) * cut], right[:, i * rest : (i + 1) * rest]], axis=1)
        for i in range(3)
    )
    return (d_inputs, gate_grad, up_grad, down_grad)


def solution(mesh):
    spec = P("row", "col")
    return jax.shard_map(
        body, mesh=mesh, in_specs=(spec,) * 7, out_specs=(spec,) * 4, check_vma=False
    )
```
